128 devices in a mesh: band: 32 (over y, z, core), lon: 4 (over x).
Axes of the slice: x: 4, y: 4, z: 4, core: 2. Of those that a mesh axis runs over, the one named last changes fastest.
Arguments:
- jacobian: bfloat16 [1048576, 137], P(('band', 'lon')), may hold values from -3 to 3
- departure: float32 [1048576], P(('band', 'lon')), may hold values from -6 to 6
- inv_var: float32 [1048576], P(('band', 'lon')), may hold values from 0.25 to 4
- frac: float32 [2, 1048576], P(None, ('band', 'lon')), may hold values from 0 to 1
- anchors: int32 [2, 1048576], P(None, ('band', 'lon')), may hold values from 0 to 1023, as said below
- counts: int32 [128, 128], P(('band', 'lon')), may hold values from 0 to 64, as said below
Outputs:
- increments: float32 [137, 1024, 512], P(None, 'band', 'lon')
The draws below stay inside these ranges and needn't reach their ends.
Inputs may be any that keep to these rules, and one draw needn't show every extreme that they name: counts[p, q] is the number of live slots among the 64 that device p holds for owner q; some pairs reach 64 in every draw, and in every draw some owner receives 64 live slots from every device. `anchors`: every slot that device p holds for owner q has its anchor in owner q's block of 32 latitude rows and 128 longitudes, and its latitude row is at most 1022.
All inputs are finite; a program needn't handle non-finite values.
Results may differ from the reference program's by a relative error of at most 0.0041.
Values may be sent and summed in bfloat16 or wider, within the bound.
A program may use at most 64 MiB of HBM per device.

```python
import math
import jax
import jax.numpy as jnp
from jax import lax

LEV = 137
LAT_DEV = 32
LON_DEV = 128
CAP = 64
SLOTS = 1048576
N_BAND = 32
N_LON = 4
DEVICES = 128


def draw_counts(key, part):
    key_width = jax.random.fold_in(key, 11)
    key_jitter = jax.random.fold_in(key, 12)
    key_amount = jax.random.fold_in(key, 13)
    key_owner = jax.random.fold_in(key, 14)
    source_dev = jnp.arange(DEVICES, dtype=jnp.int32)[:, None]
    target_dev = jnp.arange(DEVICES, dtype=jnp.int32)[None, :]
    widths = jax.random.randint(key_width, (DEVICES, 1), max(DEVICES // 8, 1), DEVICES // 2 + 1)
    jitter = jax.random.randint(key_jitter, (DEVICES, 1), 0, max(DEVICES // 16, 1) + 1)
    window_start = (source_dev + jitter) % DEVICES
    inside = (target_dev - window_start) % DEVICES < widths
    amount = jax.random.randint(key_amount, (DEVICES, DEVICES), 1, CAP + 1)
    result = jnp.where(inside, amount, 0)
    result = jnp.where(target_dev == window_start, CAP, result)
    hot_owner = jax.random.randint(key_owner, (), 0, DEVICES)
    result = jnp.where(target_dev == hot_owner, CAP, result)
    return result.astype(jnp.int32)


def draw_anchors(key, part):
    key_lat = jax.random.fold_in(key, 21)
    key_lon = jax.random.fold_in(key, 22)
    total = DEVICES * DEVICES * CAP
    slot_index = jnp.arange(total, dtype=jnp.int32)
    target_dev = slot_index // CAP % DEVICES
    band_of = target_dev // N_LON
    sector_of = target_dev % N_LON
    lat_offset = jax.random.randint(key_lat, (total,), 0, LAT_DEV)
    lat_offset = jnp.where(band_of == N_BAND - 1, jnp.minimum(lat_offset, LAT_DEV - 2), lat_offset)
    lon_offset = jax.random.randint(key_lon, (total,), 0, LON_DEV)
    lat_index = band_of * LAT_DEV + lat_offset
    lon_index = sector_of * LON_DEV + lon_offset
    return jnp.stack([lat_index, lon_index], axis=0).astype(jnp.int32)


def block_scale(rng, dims, shards, smallest, top_value):
    gain, own = 1.0, jax.random.fold_in(rng, 6)
    for dim, shards_of in shards:
        steps = jnp.exp(jax.random.uniform(jax.random.fold_in(own, dim), (shards_of,), jnp.float32, smallest / len(shards), top_value / len(shards)))
        gain = gain * jnp.repeat(steps, dims[dim] // shards_of).reshape([-1 if axis == dim else 1 for axis in range(len(dims))])
    return gain


def gaussian(key, extent, deviation, most, cuts=(), kind=jnp.bfloat16):
    level = block_scale(key, extent, cuts, -0.22, 0.18) if cuts else 1.0
    array = jax.random.normal(key, extent, jnp.float32) * deviation * level
    return jnp.minimum(jnp.maximum(array, -most), most).astype(kind)


def setup_inputs(seed: int = 0) -> dict:
    streams_of = jax.random.split(jax.random.key(seed), 7)
    jacobian = gaussian(streams_of[0], (SLOTS, LEV), 0.5, 3.0, ((0, 128),))
    departure = gaussian(streams_of[1], (SLOTS,), 1.0, 6.0, ((0, 128),), jnp.float32)
    inv_var = jnp.clip(jnp.exp(math.log(4.0) - 2.7725887 * jax.random.uniform(streams_of[2], (SLOTS,), jnp.float32) ** block_scale(streams_of[2], (SLOTS,), ((0, 128),), -0.2, 0.2)), 0.25, 4.0)
    frac = jnp.clip(1.0 * jax.random.uniform(streams_of[3], (2, SLOTS), jnp.float32) ** block_scale(streams_of[3], (2, SLOTS), ((1, 128),), -0.2, 0.2), 0.0, 1.0)
    anchors = draw_anchors(jax.random.fold_in(streams_of[6], 71), 0)
    counts = draw_counts(jax.random.fold_in(streams_of[6], 71), 0)
    return dict(jacobian=jacobian, departure=departure, inv_var=inv_var, frac=frac, anchors=anchors, counts=counts)


def reference(jacobian, departure, inv_var, frac, anchors, counts):
    devices = counts.shape[0]
    row_total = devices * CAP
    nlat = LAT_DEV * N_BAND
    nlon = LON_DEV * N_LON
    within = jnp.arange(CAP, dtype=jnp.int32)

    def one_source(grid_total, source_dev):
        first_row = (source_dev * row_total).astype(jnp.int32)
        jac_rows = lax.dynamic_slice_in_dim(jacobian, first_row, row_total, 0)
        depart_rows = lax.dynamic_slice_in_dim(departure, first_row, row_total, 0)
        inverse_rows = lax.dynamic_slice_in_dim(inv_var, first_row, row_total, 0)
        frac_rows = lax.dynamic_slice_in_dim(frac, first_row, row_total, 1)
        anchor_rows = lax.dynamic_slice_in_dim(anchors, first_row, row_total, 1)
        count_row = lax.dynamic_index_in_dim(counts, source_dev, 0, keepdims=False)
        is_live = (within[None, :] < count_row[:, None]).reshape(row_total)
        forcing = depart_rows * inverse_rows
        adjoint = jnp.where(is_live[:, None], forcing[:, None] * jac_rows.astype(jnp.float32), 0.0).astype(jnp.bfloat16)
        adjoint = lax.optimization_barrier(adjoint).astype(jnp.float32)
        lat_frac = frac_rows[0]
        lon_frac = frac_rows[1]
        corner_exprs = [(1.0 - lat_frac) * (1.0 - lon_frac), (1.0 - lat_frac) * lon_frac,
                        lat_frac * (1.0 - lon_frac), lat_frac * lon_frac]
        lat_index = anchor_rows[0]
        lon_index = anchor_rows[1]
        lon_next = (lon_index + 1) % nlon
        flat_places = [lat_index * nlon + lon_index, lat_index * nlon + lon_next,
                       (lat_index + 1) * nlon + lon_index, (lat_index + 1) * nlon + lon_next]
        for corner in range(4):
            weight = jnp.where(is_live, corner_exprs[corner], 0.0).astype(jnp.bfloat16)
            weight = lax.optimization_barrier(weight).astype(jnp.float32)
            grid_total = grid_total.at[flat_places[corner]].add(adjoint * weight[:, None])
        return grid_total, None

    grid_total = jnp.zeros((nlat * nlon, LEV), jnp.float32)
    grid_total, _ = lax.scan(one_source, grid_total, jnp.arange(devices, dtype=jnp.int32))
    return grid_total.reshape(nlat, nlon, LEV).transpose(2, 0, 1)
```

```python
import functools

import jax
import jax.numpy as jnp
from jax import lax
from jax.experimental import pallas as pl
from jax.experimental.pallas import tpu as pltpu
from jax.sharding import PartitionSpec as P

LEV = 137
LAT_DEV = 32
LON_DEV = 128
CAP = 64
ROWS = 144
HALF = ROWS // 2
GROUPS = 4
GROUP_LAT = LAT_DEV // GROUPS
WIDE = (GROUP_LAT + 2) * LON_DEV
F32 = jnp.float32
BF16 = jnp.bfloat16


def lanes(rows=1):
    return lax.broadcasted_iota(jnp.int32, (rows, 128), 1)


def pack_pair(pair, jac_ref, dep_ref, inv_ref, frac_ref, anch_ref, counts_ref):
    cols = pl.ds(pl.multiple_of(pair * 128, 128), 128)
    lane = lanes()
    first = lane < CAP
    limit = jnp.where(first, counts_ref[0, 2 * pair], counts_ref[0, 2 * pair + 1])
    live = (lane % CAP) < limit
    forcing = dep_ref[pl.ds(pair, 1), :] * inv_ref[pl.ds(pair, 1), :]
    top = jnp.where(live, jac_ref[0:136, cols].astype(F32) * forcing, 0.0)
    last = jnp.where(live, jac_ref[136:137, cols].astype(F32) * forcing, 0.0)
    a = frac_ref[0:1, cols]
    b = frac_ref[1:2, cols]
    lat = (anch_ref[0:1, cols] % LAT_DEV).astype(F32)
    lon = (anch_ref[1:2, cols] % LON_DEV).astype(F32)
    items = [last, (1.0 - a) * (1.0 - b), (1.0 - a) * b, a * (1.0 - b), a * b, lat, lon]
    row = lax.broadcasted_iota(jnp.int32, (8, 128), 0)
    tail = jnp.zeros((8, 128), F32)
    for n, item in enumerate(items):
        tail = jnp.where((row == n) & live, item, tail)
    low = top[0:HALF]
    high = jnp.concatenate([top[HALF:136], tail], axis=0)
    left = lanes(HALF) < CAP
    one = jnp.where(left, low, pltpu.roll(high, CAP, 1))
    two = jnp.where(left, pltpu.roll(low, CAP, 1), high)
    return one.astype(BF16), two.astype(BF16)


def pack_kernel(jac_ref, dep_ref, inv_ref, frac_ref, anch_ref, counts_ref, out_ref):
    def body(pair, carry):
        one, two = pack_pair(pair, jac_ref, dep_ref, inv_ref, frac_ref, anch_ref, counts_ref)
        out_ref[2 * pair] = one
        out_ref[2 * pair + 1] = two
        return carry

    lax.fori_loop(0, 64, body, 0)


def unpack_pair(one, two):
    left = lanes(HALF) < CAP
    one = one.astype(F32)
    two = two.astype(F32)
    low = jnp.where(left, one, pltpu.roll(two, CAP, 1))
    high = jnp.where(left, pltpu.roll(one, CAP, 1), two)
    return jnp.concatenate([low, high], axis=0)


def spread(slots, lhs_ref, rhs_ref, at):
    cols = pl.ds(at, 128)
    info = slots[136:144]
    w00, w01, w10, w11 = (info[n : n + 1] for n in range(1, 5))
    lat, lon = info[5:6], info[6:7]
    group = jnp.floor(lat * (1.0 / GROUP_LAT))
    inner = lat - group * GROUP_LAT
    adj = slots.astype(BF16)
    for h in range(GROUPS):
        mask = jnp.where(group == h, 1.0, 0.0).astype(BF16)
        lhs_ref[h * ROWS : (h + 1) * ROWS, cols] = adj * mask
    j = lax.broadcasted_iota(jnp.int32, (LON_DEV, 128), 0).astype(F32)
    here = j == lon
    after = j == lon + 1.0
    near = jnp.where(here, w00, jnp.where(after, w01, 0.0)).astype(BF16)
    far = jnp.where(here, w10, jnp.where(after, w11, 0.0)).astype(BF16)
    for r in range(GROUP_LAT + 1):
        on_near = jnp.where(inner == r, 1.0, 0.0).astype(BF16)
        on_far = jnp.where(inner + 1.0 == r, 1.0, 0.0).astype(BF16)
        rhs_ref[r * LON_DEV : (r + 1) * LON_DEV, cols] = near * on_near + far * on_far
    edge = lon == LON_DEV - 1.0
    r = lax.broadcasted_iota(jnp.int32, (16, 128), 0).astype(F32)
    rim = jnp.where(edge & (r == inner), w01, jnp.where(edge & (r == inner + 1.0), w11, 0.0))
    rhs_ref[(GROUP_LAT + 1) * LON_DEV : (GROUP_LAT + 1) * LON_DEV + 16, cols] = rim.astype(BF16)


def sum_kernel(depth, recv_ref, acc_ref, lhs_ref, rhs_ref):
    acc_ref[...] = jnp.zeros_like(acc_ref)
    rhs_ref[...] = jnp.zeros_like(rhs_ref)

    def body(step, carry):
        for n in range(depth // 128):
            pair = step * (depth // 128) + n
            spread(unpack_pair(recv_ref[2 * pair], recv_ref[2 * pair + 1]), lhs_ref, rhs_ref, n * 128)
        acc_ref[...] += lax.dot_general(
            lhs_ref[...], rhs_ref[...], (((1,), (1,)), ((), ())), preferred_element_type=F32
        )
        return carry

    lax.fori_loop(0, 8192 // depth, body, 0)


def halo_of(acc):
    east = acc[0, :, -LON_DEV:]
    for h in range(1, GROUPS):
        east = east + jnp.roll(acc[h, :, -LON_DEV:], h * GROUP_LAT, axis=1)
    return east, acc[GROUPS - 1, :, GROUP_LAT * LON_DEV : (GROUP_LAT + 1) * LON_DEV]


def final_kernel(acc_ref, west_ref, north_ref, corner_ref, out_ref):
    rows = acc_ref.shape[1]
    lane = lanes(rows)
    for h in range(GROUPS):
        for r in range(GROUP_LAT):
            i = h * GROUP_LAT + r
            value = acc_ref[h, :, r * LON_DEV : (r + 1) * LON_DEV]
            side = west_ref[:, i : i + 1]
            if r == 0 and h > 0:
                value = value + acc_ref[h - 1, :, GROUP_LAT * LON_DEV : (GROUP_LAT + 1) * LON_DEV]
            if i == 0:
                value = value + north_ref[...]
                side = side + corner_ref[:, LAT_DEV : LAT_DEV + 1]
            value = value + jnp.where(lane == 0, side, 0.0)
            out_ref[pl.ds(i, rows, stride=LAT_DEV), :] = value


def per_device(jacobian, departure, inv_var, frac, anchors, counts):
    vmem = pl.BlockSpec(memory_space=pltpu.VMEM)
    packed = pl.pallas_call(
        pack_kernel,
        out_shape=jax.ShapeDtypeStruct((128, HALF, 128), BF16),
        in_specs=[vmem] * 5 + [pl.BlockSpec(memory_space=pltpu.SMEM)],
        out_specs=vmem,
        name="pack",
    )(jacobian.T, departure.reshape(64, 128), inv_var.reshape(64, 128), frac, anchors, counts)
    received = lax.all_to_all(packed, ("band", "lon"), split_axis=0, concat_axis=0, tiled=True)
    depth = 512
    acc = pl.pallas_call(
        functools.partial(sum_kernel, depth),
        out_shape=jax.ShapeDtypeStruct((GROUPS * ROWS, WIDE), F32),
        in_specs=[vmem],
        out_specs=vmem,
        scratch_shapes=[pltpu.VMEM((GROUPS * ROWS, depth), BF16), pltpu.VMEM((WIDE, depth), BF16)],
        compiler_params=pltpu.CompilerParams(vmem_limit_bytes=40 * 2**20),
        name="sums",
    )(received).reshape(GROUPS, ROWS, WIDE)
    east, south = halo_of(acc)
    bands, lons = lax.axis_size("band"), lax.axis_size("lon")
    to_east = [(i, (i + 1) % lons) for i in range(lons)]
    to_south = [(i, i + 1) for i in range(bands - 1)]
    west = lax.ppermute(east, "lon", to_east)
    north = lax.ppermute(south, "band", to_south)
    corner = lax.ppermute(west, "band", to_south)
    block = 48
    out = pl.pallas_call(
        final_kernel,
        grid=(ROWS // block,),
        out_shape=jax.ShapeDtypeStruct((LEV * LAT_DEV, LON_DEV), F32),
        in_specs=[pl.BlockSpec((GROUPS, block, WIDE), lambda n: (0, n, 0))]
        + [pl.BlockSpec((block, LON_DEV), lambda n: (n, 0))] * 3,
        out_specs=pl.BlockSpec((block * LAT_DEV, LON_DEV), lambda n: (n, 0)),
        name="final",
    )(acc, west, north, corner)
    return out.reshape(LEV, LAT_DEV, LON_DEV)


def solution(mesh):
    return jax.shard_map(
        per_device,
        mesh=mesh,
        in_specs=(
            P(("band", "lon"), None),
            P(("band", "lon")),
            P(("band", "lon")),
            P(None, ("band", "lon")),
            P(None, ("band", "lon")),
            P(("band", "lon"), None),
        ),
        out_specs=P(None, "band", "lon"),
        check_vma=False,
    )
```

```python
import jax
import jax.numpy as jnp
from jax import lax
from jax.experimental import pallas as pl
from jax.experimental.pallas import tpu as pltpu
from jax.sharding import PartitionSpec as P

LEV = 137
LAT_DEV = 32
LON_DEV = 128
CAP = 64
ROWS = 144
HALF = ROWS // 2
GROUPS = 4
GROUP_LAT = LAT_DEV // GROUPS
WIDE = (GROUP_LAT + 2) * LON_DEV
F32 = jnp.float32
BF16 = jnp.bfloat16
MESH = pl.DeviceIdType.MESH
DEPTH = 512


def lanes(rows=1):
    return lax.broadcasted_iota(jnp.int32, (rows, 128), 1)


def pack_pair(pair, jac_ref, dep_ref, inv_ref, frac_ref, anch_ref, counts_ref):
    cols = pl.ds(pl.multiple_of(pair * 128, 128), 128)
    lane = lanes()
    first = lane < CAP
    limit = jnp.where(first, counts_ref[0, 2 * pair], counts_ref[0, 2 * pair + 1])
    live = (lane % CAP) < limit
    forcing = dep_ref[pl.ds(pair, 1), :] * inv_ref[pl.ds(pair, 1), :]
    top = jnp.where(live, jac_ref[0:136, cols].astype(F32) * forcing, 0.0)
    last = jnp.where(live, jac_ref[136:137, cols].astype(F32) * forcing, 0.0)
    a = frac_ref[0:1, cols]
    b = frac_ref[1:2, cols]
    lat = (anch_ref[0:1, cols] % LAT_DEV).astype(F32)
    lon = (anch_ref[1:2, cols] % LON_DEV).astype(F32)
    items = [last, (1.0 - a) * (1.0 - b), (1.0 - a) * b, a * (1.0 - b), a * b, lat, lon]
    row = lax.broadcasted_iota(jnp.int32, (8, 128), 0)
    tail = jnp.zeros((8, 128), F32)
    for n, item in enumerate(items):
        tail = jnp.where((row == n) & live, item, tail)
    low = top[0:HALF]
    high = jnp.concatenate([top[HALF:136], tail], axis=0)
    left = lanes(HALF) < CAP
    one = jnp.where(left, low, pltpu.roll(high, CAP, 1))
    two = jnp.where(left, pltpu.roll(low, CAP, 1), high)
    return one.astype(BF16), two.astype(BF16)


def unpack_pair(one, two):
    left = lanes(HALF) < CAP
    one = one.astype(F32)
    two = two.astype(F32)
    low = jnp.where(left, one, pltpu.roll(two, CAP, 1))
    high = jnp.where(left, pltpu.roll(one, CAP, 1), two)
    return jnp.concatenate([low, high], axis=0)


def spread(slots, lhs_ref, rhs_ref, at):
    cols = pl.ds(at, 128)
    info = slots[136:144]
    w00, w01, w10, w11 = (info[n : n + 1] for n in range(1, 5))
    lat, lon = info[5:6], info[6:7]
    group = jnp.floor(lat * (1.0 / GROUP_LAT))
    inner = lat - group * GROUP_LAT
    adj = slots.astype(BF16)
    for h in range(GROUPS):
        mask = jnp.where(group == h, 1.0, 0.0).astype(BF16)
        lhs_ref[h * ROWS : (h + 1) * ROWS, cols] = adj * mask
    j = lax.broadcasted_iota(jnp.int32, (LON_DEV, 128), 0).astype(F32)
    here = j == lon
    after = j == lon + 1.0
    near = jnp.where(here, w00, jnp.where(after, w01, 0.0)).astype(BF16)
    far = jnp.where(here, w10, jnp.where(after, w11, 0.0)).astype(BF16)
    for r in range(GROUP_LAT + 1):
        on_near = jnp.where(inner == r, 1.0, 0.0).astype(BF16)
        on_far = jnp.where(inner + 1.0 == r, 1.0, 0.0).astype(BF16)
        rhs_ref[r * LON_DEV : (r + 1) * LON_DEV, cols] = near * on_near + far * on_far
    edge = lon == LON_DEV - 1.0
    r = lax.broadcasted_iota(jnp.int32, (16, 128), 0).astype(F32)
    rim = jnp.where(edge & (r == inner), w01, jnp.where(edge & (r == inner + 1.0), w11, 0.0))
    rhs_ref[(GROUP_LAT + 1) * LON_DEV : (GROUP_LAT + 1) * LON_DEV + 16, cols] = rim.astype(BF16)


def place():
    band, lon = lax.axis_index("band"), lax.axis_index("lon")
    return lon, band // 8, band // 2 % 4, band % 2


def band_of(y, z, core):
    return (y * 4 + z) * 2 + core


def stage_one(n):
    return n % 4 * (1 - n // 4), (n % 4 + 1) * (n // 4) % 4, n // 7


def stage_two(n):
    return n % 3 + 1, (n // 3 + 1) % 4, n // 9


def stage_three(n):
    return n % 4, n // 4 + 1, 1


STAGES = ((stage_one, 0, 8), (stage_two, 8, 12), (stage_three, 20, 12))


def main_kernel(
    jac_hbm, dep_ref, inv_ref, frac_ref, anch_ref, counts_ref,
    acc_ref, west_out, north_out, corner_out,
    jac_ref, packed, recv, lhs_ref, rhs_ref, east, south, west, north, corner,
    jac_sem, own_sem, send_sem, recv_sem, halo_send, halo_recv, x_sem, y_sem, core_sem,
):
    x, y, z, core = place()
    barrier = pltpu.get_barrier_semaphore()
    x_line = [(band_of(y, z, core), (x + d) % 4) for d in (1, 3, 2)]
    y_line = [(band_of((y + d) % 4, z, core), x) for d in (1, 3, 2)]
    z_line = [(band_of(y, (z + d) % 4, core), x) for d in (1, 3, 2)]
    partner = [(band_of(y, z, 1 - core), x)]

    def greet(sem, devices):
        for device in devices:
            pl.semaphore_signal(sem, inc=1, device_id=device, device_id_type=MESH)

    def owner_band(stage, n):
        dy, dz, dc = stage(n)
        return band_of((y + dy) % 4, (z + dz) % 4, (core + dc) % 2)

    def pack(stage, base, first, last):
        def body(n, carry):
            band = owner_band(stage, n)
            for half in range(2):
                one, two = pack_pair(
                    2 * band + half, jac_ref, dep_ref, inv_ref, frac_ref, anch_ref, counts_ref
                )
                packed[(base + n) * 4 + 2 * half] = one
                packed[(base + n) * 4 + 2 * half + 1] = two
            return carry

        lax.fori_loop(first, last, body, 0)

    def block_copy(slot, target, source_x, device):
        return pltpu.make_async_remote_copy(
            src_ref=packed.at[slot * 4 + target],
            dst_ref=recv.at[slot * 4 + source_x],
            send_sem=send_sem.at[slot * 4 + target],
            recv_sem=recv_sem.at[slot * 4 + source_x],
            device_id=device,
            device_id_type=MESH,
        )

    def send(stage, base, first, last):
        def body(n, carry):
            band = owner_band(stage, n)
            for d in range(4):
                target = (x + d) % 4
                block_copy(base + n, target, x, (band, target)).start()
            return carry

        lax.fori_loop(first, last, body, 0)

    greet(barrier, x_line + y_line + z_line + partner)
    load = pltpu.make_async_copy(jac_hbm, jac_ref, jac_sem)
    load.start()
    acc_ref[...] = jnp.zeros_like(acc_ref)
    rhs_ref[...] = jnp.zeros_like(rhs_ref)
    load.wait()
    (one, _, _), (two, two_base, _), (three, three_base, _) = STAGES
    pack(one, 0, 0, 8)
    pack(two, two_base, 0, 4)
    pl.semaphore_wait(barrier, 10)
    greet(x_sem, x_line)
    pack(two, two_base, 4, 12)
    pl.semaphore_wait(x_sem, 3)
    greet(y_sem, y_line)
    own = pltpu.make_async_copy(packed.at[x], recv.at[x], own_sem)
    own.start()
    for d in (1, 3, 2):
        target = (x + d) % 4
        block_copy(0, target, x, (band_of(y, z, core), target)).start()
    send(one, 0, 1, 8)
    pack(three, three_base, 0, 12)
    pl.semaphore_wait(y_sem, 3)
    greet(core_sem, partner)
    send(two, two_base, 0, 12)
    pl.semaphore_wait(core_sem, 1)
    send(three, three_base, 0, 12)

    def arrived(slot, source_x):
        block_copy(slot, source_x, source_x, x_line[0]).wait_recv()

    own.wait()
    for d in (1, 3, 2):
        arrived(0, (x + d) % 4)

    def body(step, carry):
        for n in range(DEPTH // 256):
            slot = step * (DEPTH // 256) + n

            @pl.when(slot > 0)
            def _():
                for source in range(4):
                    arrived(slot, source)

            for half in range(2):
                at = slot * 4 + 2 * half
                spread(unpack_pair(recv[at], recv[at + 1]), lhs_ref, rhs_ref, n * 256 + half * 128)
        acc_ref[...] += lax.dot_general(
            lhs_ref[...], rhs_ref[...], (((1,), (1,)), ((), ())), preferred_element_type=F32
        )
        return carry

    lax.fori_loop(0, 8192 // DEPTH, body, 0)

    rim = pl.ds(WIDE - LON_DEV, LON_DEV)
    total = acc_ref[0:ROWS, rim]
    for h in range(1, GROUPS):
        total = total + pltpu.roll(acc_ref[h * ROWS : (h + 1) * ROWS, rim], h * GROUP_LAT, 1)
    east[...] = total
    south[...] = acc_ref[(GROUPS - 1) * ROWS : GROUPS * ROWS, pl.ds(WIDE - 2 * LON_DEV, LON_DEV)]
    next_band = (band_of(y, z, core) + 1) % 32
    halos = []
    for n, (source, landing, device) in enumerate(
        [
            (south, north, (next_band, x)),
            (east, corner, (next_band, (x + 1) % 4)),
            (east, west, (band_of(y, z, core), (x + 1) % 4)),
        ]
    ):
        halos.append(
            pltpu.make_async_remote_copy(
                src_ref=source,
                dst_ref=landing,
                send_sem=halo_send.at[n],
                recv_sem=halo_recv.at[n],
                device_id=device,
                device_id_type=MESH,
            )
        )
    for copy in halos:
        copy.start()

    def drain(n, carry):
        slot = n // 4
        block_copy(slot, n % 4, x, x_line[0]).wait_send()
        return carry

    for d in (1, 3, 2):
        block_copy(0, (x + d) % 4, x, x_line[0]).wait_send()
    lax.fori_loop(4, 128, drain, 0)
    for copy in halos:
        copy.wait()
    west_out[...] = west[...]
    north_out[...] = north[...]
    corner_out[...] = corner[...]


def final_kernel(acc_ref, west_ref, north_ref, corner_ref, out_ref):
    rows = acc_ref.shape[1]
    lane = lanes(rows)
    for h in range(GROUPS):
        for r in range(GROUP_LAT):
            i = h * GROUP_LAT + r
            value = acc_ref[h, :, r * LON_DEV : (r + 1) * LON_DEV]
            side = west_ref[:, i : i + 1]
            if r == 0 and h > 0:
                value = value + acc_ref[h - 1, :, GROUP_LAT * LON_DEV : (GROUP_LAT + 1) * LON_DEV]
            if i == 0:
                value = value + north_ref[...]
                side = side + corner_ref[:, LAT_DEV : LAT_DEV + 1]
            value = value + jnp.where(lane == 0, side, 0.0)
            out_ref[pl.ds(i, rows, stride=LAT_DEV), :] = value


def per_device(jacobian, departure, inv_var, frac, anchors, counts):
    vmem = pl.BlockSpec(memory_space=pltpu.VMEM)
    halo = jax.ShapeDtypeStruct((ROWS, LON_DEV), F32)
    acc, west, north, corner = pl.pallas_call(
        main_kernel,
        out_shape=[jax.ShapeDtypeStruct((GROUPS * ROWS, WIDE), F32), halo, halo, halo],
        in_specs=[pl.BlockSpec(memory_space=pl.ANY)]
        + [vmem] * 4
        + [pl.BlockSpec(memory_space=pltpu.SMEM)],
        out_specs=[vmem] * 4,
        scratch_shapes=[
            pltpu.VMEM((LEV, 8192), BF16),
            pltpu.VMEM((128, HALF, 128), BF16),
            pltpu.VMEM((128, HALF, 128), BF16),
            pltpu.VMEM((GROUPS * ROWS, DEPTH), BF16),
            pltpu.VMEM((WIDE, DEPTH), BF16),
        ]
        + [pltpu.VMEM((ROWS, LON_DEV), F32)] * 5
        + [
            pltpu.SemaphoreType.DMA,
            pltpu.SemaphoreType.DMA,
            pltpu.SemaphoreType.DMA((128,)),
            pltpu.SemaphoreType.DMA((128,)),
            pltpu.SemaphoreType.DMA((3,)),
            pltpu.SemaphoreType.DMA((3,)),
            pltpu.SemaphoreType.REGULAR,
            pltpu.SemaphoreType.REGULAR,
            pltpu.SemaphoreType.REGULAR,
        ],
        compiler_params=pltpu.CompilerParams(
            collective_id=0, has_side_effects=True, vmem_limit_bytes=40 * 2**20
        ),
        name="exchange",
    )(jacobian.T, departure.reshape(64, 128), inv_var.reshape(64, 128), frac, anchors, counts)
    acc = acc.reshape(GROUPS, ROWS, WIDE)
    block = 48
    out = pl.pallas_call(
        final_kernel,
        grid=(ROWS // block,),
        out_shape=jax.ShapeDtypeStruct((LEV * LAT_DEV, LON_DEV), F32),
        in_specs=[pl.BlockSpec((GROUPS, block, WIDE), lambda n: (0, n, 0))]
        + [pl.BlockSpec((block, LON_DEV), lambda n: (n, 0))] * 3,
        out_specs=pl.BlockSpec((block * LAT_DEV, LON_DEV), lambda n: (n, 0)),
        name="final",
    )(acc, west, north, corner)
    return out.reshape(LEV, LAT_DEV, LON_DEV)


def solution(mesh):
    return jax.shard_map(
        per_device,
        mesh=mesh,
        in_specs=(
            P(("band", "lon"), None),
            P(("band", "lon")),
            P(("band", "lon")),
            P(None, ("band", "lon")),
            P(None, ("band", "lon")),
            P(("band", "lon"), None),
        ),
        out_specs=P(None, "band", "lon"),
        check_vma=False,
    )
```

```python
import jax
import jax.numpy as jnp
from jax import lax
from jax.experimental import pallas as pl
from jax.experimental.pallas import tpu as pltpu
from jax.sharding import PartitionSpec as P

LEV = 137
LAT_DEV = 32
LON_DEV = 128
CAP = 64
ROWS = 144
HALF = ROWS // 2
GROUPS = 4
GROUP_LAT = LAT_DEV // GROUPS
WIDE = (GROUP_LAT + 2) * LON_DEV
F32 = jnp.float32
BF16 = jnp.bfloat16
MESH = pl.DeviceIdType.MESH
DEPTH = 256
BLOCKS = DEPTH // CAP


def lanes(rows=1):
    return lax.broadcasted_iota(jnp.int32, (rows, 128), 1)


def pack_pair(pair, jac_ref, dep_ref, inv_ref, frac_ref, anch_ref, counts_ref):
    cols = pl.ds(pl.multiple_of(pair * 128, 128), 128)
    lane = lanes()
    first = lane < CAP
    limit = jnp.where(first, counts_ref[0, 2 * pair], counts_ref[0, 2 * pair + 1])
    live = (lane % CAP) < limit
    forcing = dep_ref[pl.ds(pair, 1), :] * inv_ref[pl.ds(pair, 1), :]
    top = jnp.where(live, jac_ref[0:136, cols].astype(F32) * forcing, 0.0)
    last = jnp.where(live, jac_ref[136:137, cols].astype(F32) * forcing, 0.0)
    a = frac_ref[0:1, cols]
    b = frac_ref[1:2, cols]
    lat = (anch_ref[0:1, cols] % LAT_DEV).astype(F32)
    lon = (anch_ref[1:2, cols] % LON_DEV).astype(F32)
    items = [last, (1.0 - a) * (1.0 - b), (1.0 - a) * b, a * (1.0 - b), a * b, lat, lon]
    row = lax.broadcasted_iota(jnp.int32, (8, 128), 0)
    tail = jnp.zeros((8, 128), F32)
    for n, item in enumerate(items):
        tail = jnp.where((row == n) & live, item, tail)
    low = top[0:HALF]
    high = jnp.concatenate([top[HALF:136], tail], axis=0)
    left = lanes(HALF) < CAP
    one = jnp.where(left, low, pltpu.roll(high, CAP, 1))
    two = jnp.where(left, pltpu.roll(low, CAP, 1), high)
    return one.astype(BF16), two.astype(BF16)


def unpack_pair(one, two):
    left = lanes(HALF) < CAP
    one = one.astype(F32)
    two = two.astype(F32)
    low = jnp.where(left, one, pltpu.roll(two, CAP, 1))
    high = jnp.where(left, pltpu.roll(one, CAP, 1), two)
    return jnp.concatenate([low, high], axis=0)


def spread(slots, lhs_ref, rhs_ref, at):
    cols = pl.ds(at, 128)
    info = slots[136:144]
    w00, w01, w10, w11 = (info[n : n + 1] for n in range(1, 5))
    lat, lon = info[5:6], info[6:7]
    group = jnp.floor(lat * (1.0 / GROUP_LAT))
    inner = lat - group * GROUP_LAT
    adj = slots.astype(BF16)
    for h in range(GROUPS):
        mask = jnp.where(group == h, 1.0, 0.0).astype(BF16)
        lhs_ref[h * ROWS : (h + 1) * ROWS, cols] = adj * mask
    j = lax.broadcasted_iota(jnp.int32, (LON_DEV, 128), 0).astype(F32)
    here = j == lon
    after = j == lon + 1.0
    near = jnp.where(here, w00, jnp.where(after, w01, 0.0)).astype(BF16)
    far = jnp.where(here, w10, jnp.where(after, w11, 0.0)).astype(BF16)
    for r in range(GROUP_LAT + 1):
        on_near = jnp.where(inner == r, 1.0, 0.0).astype(BF16)
        on_far = jnp.where(inner + 1.0 == r, 1.0, 0.0).astype(BF16)
        rhs_ref[r * LON_DEV : (r + 1) * LON_DEV, cols] = near * on_near + far * on_far
    edge = lon == LON_DEV - 1.0
    r = lax.broadcasted_iota(jnp.int32, (16, 128), 0).astype(F32)
    rim = jnp.where(edge & (r == inner), w01, jnp.where(edge & (r == inner + 1.0), w11, 0.0))
    rhs_ref[(GROUP_LAT + 1) * LON_DEV : (GROUP_LAT + 1) * LON_DEV + 16, cols] = rim.astype(BF16)


def place():
    band, lon = lax.axis_index("band"), lax.axis_index("lon")
    return lon, band // 8, band // 2 % 4, band % 2


def band_of(y, z, core):
    return (y * 4 + z) * 2 + core


ORDER = (
    (0, 0, 0, 0, 0),
    (0, 0, 0, 1, 1),
    (2, 2, 0, 0, 5),
    (2, 3, 0, 0, 4),
    (0, 1, 0, 0, 6),
    (3, 2, 0, 0, 8),
    (1, 0, 0, 0, 2),
    (1, 2, 0, 0, 10),
    (3, 0, 0, 0, 3),
    (2, 1, 0, 0, 12),
    (0, 3, 0, 0, 7),
    (1, 1, 0, 0, 11),
    (3, 3, 0, 0, 9),
    (3, 1, 0, 0, 16),
    (1, 3, 0, 0, 13),
    (2, 0, 0, 0, 14),
    (0, 2, 0, 0, 15),
    (0, 0, 2, 0, 98),
    (0, 0, 3, 0, 85),
    (0, 0, 1, 0, 91),
    (2, 2, 2, 0, 20),
    (3, 2, 2, 0, 19),
    (1, 0, 2, 0, 17),
    (1, 2, 2, 0, 21),
    (3, 0, 2, 0, 18),
    (2, 3, 2, 0, 23),
    (0, 1, 2, 0, 37),
    (2, 1, 2, 0, 26),
    (0, 3, 2, 0, 95),
    (3, 3, 2, 0, 22),
    (1, 1, 2, 0, 24),
    (3, 1, 2, 0, 27),
    (1, 3, 2, 0, 28),
    (2, 2, 3, 0, 30),
    (2, 2, 1, 0, 31),
    (0, 2, 2, 0, 48),
    (2, 0, 2, 0, 35),
    (2, 3, 3, 0, 33),
    (0, 1, 1, 0, 64),
    (2, 1, 1, 0, 32),
    (0, 3, 3, 0, 92),
    (1, 2, 3, 0, 39),
    (3, 0, 1, 0, 25),
    (3, 2, 1, 0, 38),
    (1, 0, 3, 0, 29),
    (2, 3, 1, 0, 40),
    (0, 1, 3, 0, 82),
    (3, 2, 3, 0, 41),
    (1, 0, 1, 0, 34),
    (2, 1, 3, 0, 44),
    (0, 3, 1, 0, 94),
    (1, 2, 1, 0, 43),
    (3, 0, 3, 0, 36),
    (1, 1, 1, 0, 42),
    (3, 3, 3, 0, 45),
    (1, 1, 3, 0, 51),
    (3, 3, 1, 0, 46),
    (0, 2, 3, 0, 63),
    (2, 0, 1, 0, 47),
    (1, 3, 3, 0, 52),
    (3, 1, 1, 0, 50),
    (3, 1, 3, 0, 55),
    (1, 3, 1, 0, 54),
    (2, 0, 3, 0, 56),
    (0, 2, 1, 0, 74),
    (2, 2, 2, 1, 60),
    (2, 2, 3, 1, 58),
    (0, 0, 1, 1, 109),
    (2, 1, 2, 1, 61),
    (0, 3, 0, 1, 90),
    (1, 2, 2, 1, 66),
    (3, 0, 0, 1, 49),
    (2, 2, 1, 1, 62),
    (0, 0, 3, 1, 96),
    (2, 3, 2, 1, 68),
    (0, 1, 0, 1, 87),
    (3, 2, 2, 1, 69),
    (1, 0, 0, 1, 53),
    (1, 2, 1, 1, 75),
    (3, 0, 3, 1, 59),
    (2, 3, 3, 1, 70),
    (0, 1, 1, 1, 108),
    (0, 2, 2, 1, 111),
    (2, 0, 0, 1, 57),
    (2, 2, 0, 1, 67),
    (0, 0, 2, 1, 126),
    (2, 1, 1, 1, 71),
    (0, 3, 3, 1, 93),
    (2, 0, 2, 1, 78),
    (0, 2, 0, 1, 110),
    (2, 1, 3, 1, 77),
    (0, 3, 1, 1, 112),
    (1, 1, 2, 1, 79),
    (3, 3, 0, 1, 65),
    (3, 2, 3, 1, 84),
    (1, 0, 1, 1, 72),
    (2, 3, 1, 1, 81),
    (0, 1, 3, 1, 113),
    (1, 2, 3, 1, 88),
    (3, 0, 1, 1, 73),
    (3, 2, 1, 1, 89),
    (1, 0, 3, 1, 80),
    (3, 3, 2, 1, 99),
    (1, 1, 0, 1, 76),
    (1, 3, 2, 1, 102),
    (3, 1, 0, 1, 83),
    (3, 1, 2, 1, 104),
    (1, 3, 0, 1, 86),
    (3, 3, 3, 1, 101),
    (1, 1, 1, 1, 100),
    (1, 0, 2, 1, 105),
    (3, 2, 0, 1, 97),
    (0, 2, 3, 1, 114),
    (2, 0, 1, 1, 103),
    (1, 1, 3, 1, 107),
    (3, 3, 1, 1, 106),
    (0, 2, 1, 1, 117),
    (2, 0, 3, 1, 118),
    (2, 3, 0, 1, 115),
    (0, 1, 2, 1, 123),
    (3, 1, 3, 1, 119),
    (1, 3, 1, 1, 121),
    (0, 3, 2, 1, 127),
    (2, 1, 0, 1, 116),
    (3, 1, 1, 1, 122),
    (1, 3, 3, 1, 124),
    (3, 0, 2, 1, 125),
    (1, 2, 0, 1, 120),
)


def main_kernel(
    jac_hbm, dep_hbm, inv_hbm, frac_hbm, anch_hbm, counts_hbm,
    out_ref,
    jac_ref, dep_ref, inv_ref, frac_ref, anch_ref, counts_ref, acc_ref, packed, recv, lhs_even, rhs_even, lhs_odd, rhs_odd, east, south, west, north, corner,
    load_sem, own_sem, send_sem, recv_sem, halo_send, halo_recv, z_sem, core_sem,
):
    x, y, z, core = place()
    barrier = pltpu.get_barrier_semaphore()
    plane = [
        (band_of((y + dy) % 4, z, core), (x + dx) % 4)
        for dx, dy in sorted({(n % 4, n // 4) for n in range(1, 16)})
    ]
    z_line = [(band_of(y, (z + d) % 4, core), x) for d in (1, 3, 2)]
    partner = [(band_of(y, z, 1 - core), x)]

    def greet(sem, devices):
        for device in devices:
            pl.semaphore_signal(sem, inc=1, device_id=device, device_id_type=MESH)

    def pack(first, last):
        def body(n, carry):
            band = band_of((y + n) % 4, (z + n // 4) % 4, (core + n // 16) % 2)
            for half in range(2):
                one, two = pack_pair(
                    2 * band + half, jac_ref, dep_ref, inv_ref, frac_ref, anch_ref, counts_ref
                )
                packed[n * 4 + 2 * half] = one
                packed[n * 4 + 2 * half + 1] = two
            return carry

        lax.fori_loop(first, last, body, 0)

    def block_copy(n):
        dx, dy, dz, dc, slot = ORDER[n]
        target = (x + dx) % 4
        return pltpu.make_async_remote_copy(
            src_ref=packed.at[(dc * 16 + dz * 4 + dy) * 4 + target],
            dst_ref=recv.at[slot],
            send_sem=send_sem.at[slot],
            recv_sem=recv_sem.at[slot],
            device_id=(band_of((y + dy) % 4, (z + dz) % 4, (core + dc) % 2), target),
            device_id_type=MESH,
        )

    def send(first, last):
        for n in range(first, last):
            block_copy(n).start()

    greet(barrier, plane + z_line + partner)
    loads = [
        pltpu.make_async_copy(source, held, load_sem.at[n])
        for n, (source, held) in enumerate(
            [
                (counts_hbm, counts_ref),
                (dep_hbm, dep_ref),
                (inv_hbm, inv_ref),
                (frac_hbm, frac_ref),
                (anch_hbm, anch_ref),
                (jac_hbm, jac_ref),
            ]
        )
    ]
    for load in loads:
        load.start()
    acc_ref[...] = jnp.zeros_like(acc_ref)
    for held in (rhs_even, rhs_odd):
        held[...] = jnp.zeros_like(held)
    for load in loads:
        load.wait()
    pack(0, 17)
    pl.semaphore_wait(barrier, 19)
    greet(z_sem, z_line)
    send(1, 17)
    pack(17, 22)
    pl.semaphore_wait(z_sem, 3)
    greet(core_sem, partner)
    send(17, 65)
    pl.semaphore_wait(core_sem, 1)
    pack(22, 32)
    own = pltpu.make_async_copy(packed.at[x], recv.at[0], own_sem)
    own.start()
    send(65, 128)

    def arrived(slot):
        pltpu.make_async_remote_copy(
            src_ref=packed.at[slot],
            dst_ref=recv.at[slot],
            send_sem=send_sem.at[slot],
            recv_sem=recv_sem.at[slot],
            device_id=partner[0],
            device_id_type=MESH,
        ).wait_recv()

    def fill(step, lhs_ref, rhs_ref, first=0):
        for n in range(first, BLOCKS):
            arrived(step * BLOCKS + n)
        for n in range(0, BLOCKS, 2):
            at = step * BLOCKS + n
            spread(unpack_pair(recv[at], recv[at + 1]), lhs_ref, rhs_ref, n * CAP)

    def add(lhs_ref, rhs_ref):
        acc_ref[...] += lax.dot_general(
            lhs_ref[...], rhs_ref[...], (((1,), (1,)), ((), ())), preferred_element_type=F32
        )

    own.wait()
    fill(0, lhs_even, rhs_even, 1)

    def body(t, carry):
        fill(2 * t + 1, lhs_odd, rhs_odd)
        add(lhs_even, rhs_even)
        fill(2 * t + 2, lhs_even, rhs_even)
        add(lhs_odd, rhs_odd)
        return carry

    lax.fori_loop(0, 8192 // DEPTH // 2 - 1, body, 0)
    add(lhs_even, rhs_even)
    fill(8192 // DEPTH - 1, lhs_odd, rhs_odd)
    add(lhs_odd, rhs_odd)

    rim = pl.ds(WIDE - LON_DEV, LON_DEV)
    total = acc_ref[0:ROWS, rim]
    for h in range(1, GROUPS):
        total = total + pltpu.roll(acc_ref[h * ROWS : (h + 1) * ROWS, rim], h * GROUP_LAT, 1)
    east[...] = total
    south[...] = acc_ref[(GROUPS - 1) * ROWS : GROUPS * ROWS, pl.ds(WIDE - 2 * LON_DEV, LON_DEV)]
    next_band = (band_of(y, z, core) + 1) % 32
    halos = []
    for n, (source, landing, device) in enumerate(
        [
            (south, north, (next_band, x)),
            (east, corner, (next_band, (x + 1) % 4)),
            (east, west, (band_of(y, z, core), (x + 1) % 4)),
        ]
    ):
        halos.append(
            pltpu.make_async_remote_copy(
                src_ref=source,
                dst_ref=landing,
                send_sem=halo_send.at[n],
                recv_sem=halo_recv.at[n],
                device_id=device,
                device_id_type=MESH,
            )
        )
    for copy in halos:
        copy.start()

    def own_row(i):
        h, r = i // GROUP_LAT, i % GROUP_LAT
        value = acc_ref[h * ROWS : (h + 1) * ROWS, r * LON_DEV : (r + 1) * LON_DEV]
        if r == 0 and h > 0:
            value = value + acc_ref[
                (h - 1) * ROWS : h * ROWS, GROUP_LAT * LON_DEV : (GROUP_LAT + 1) * LON_DEV
            ]
        return value

    def drain(slot, carry):
        pltpu.make_async_remote_copy(
            src_ref=packed.at[slot],
            dst_ref=recv.at[slot],
            send_sem=send_sem.at[slot],
            recv_sem=recv_sem.at[slot],
            device_id=partner[0],
            device_id_type=MESH,
        ).wait_send()
        return carry

    lax.fori_loop(1, 128, drain, 0)
    for copy in halos:
        copy.wait()
    lane = lanes(LEV)
    for i in range(LAT_DEV):
        value = own_row(i)[0:LEV]
        side = west[0:LEV, i : i + 1]
        if i == 0:
            value = value + north[0:LEV]
            side = side + corner[0:LEV, LAT_DEV : LAT_DEV + 1]
        out_ref[pl.ds(i, LEV, stride=LAT_DEV), :] = value + jnp.where(lane == 0, side, 0.0)


def per_device(jacobian, departure, inv_var, frac, anchors, counts):
    out = pl.pallas_call(
        main_kernel,
        out_shape=jax.ShapeDtypeStruct((LEV * LAT_DEV, LON_DEV), F32),
        in_specs=[pl.BlockSpec(memory_space=pltpu.HBM)] * 6,
        out_specs=pl.BlockSpec(memory_space=pltpu.VMEM),
        scratch_shapes=[
            pltpu.VMEM((LEV, 8192), BF16),
            pltpu.VMEM((64, 128), F32),
            pltpu.VMEM((64, 128), F32),
            pltpu.VMEM((2, 8192), F32),
            pltpu.VMEM((2, 8192), jnp.int32),
            pltpu.SMEM((1, 128), jnp.int32),
            pltpu.VMEM((GROUPS * ROWS, WIDE), F32),
            pltpu.VMEM((128, HALF, 128), BF16),
            pltpu.VMEM((128, HALF, 128), BF16),
            pltpu.VMEM((GROUPS * ROWS, DEPTH), BF16),
            pltpu.VMEM((WIDE, DEPTH), BF16),
            pltpu.VMEM((GROUPS * ROWS, DEPTH), BF16),
            pltpu.VMEM((WIDE, DEPTH), BF16),
        ]
        + [pltpu.VMEM((ROWS, LON_DEV), F32)] * 5
        + [
            pltpu.SemaphoreType.DMA((6,)),
            pltpu.SemaphoreType.DMA,
            pltpu.SemaphoreType.DMA((128,)),
            pltpu.SemaphoreType.DMA((128,)),
            pltpu.SemaphoreType.DMA((3,)),
            pltpu.SemaphoreType.DMA((3,)),
            pltpu.SemaphoreType.REGULAR,
            pltpu.SemaphoreType.REGULAR,
        ],
        compiler_params=pltpu.CompilerParams(
            collective_id=0, has_side_effects=True, vmem_limit_bytes=40 * 2**20
        ),
        name="exchange",
    )(
        *(
            pltpu.with_memory_space_constraint(value, pltpu.HBM)
            for value in (
                jacobian.T,
                departure.reshape(64, 128),
                inv_var.reshape(64, 128),
                frac,
                anchors,
                counts,
            )
        )
    )
    return out.reshape(LEV, LAT_DEV, LON_DEV)


def solution(mesh):
    return jax.shard_map(
        per_device,
        mesh=mesh,
        in_specs=(
            P(("band", "lon"), None),
            P(("band", "lon")),
            P(("band", "lon")),
            P(None, ("band", "lon")),
            P(None, ("band", "lon")),
            P(("band", "lon"), None),
        ),
        out_specs=P(None, "band", "lon"),
        check_vma=False,
    )
```

```python
import jax
import jax.numpy as jnp
from jax import lax
from jax.experimental import pallas as pl
from jax.experimental.pallas import tpu as pltpu
from jax.sharding import PartitionSpec as P

LEV = 137
LAT_DEV = 32
LON_DEV = 128
CAP = 64
ROWS = 144
HALF = ROWS // 2
GROUPS = 4
GROUP_LAT = LAT_DEV // GROUPS
WIDE = (GROUP_LAT + 2) * LON_DEV
F32 = jnp.float32
BF16 = jnp.bfloat16
MESH = pl.DeviceIdType.MESH
CONTRACT = (((1,), (1,)), ((), ()))
DEPTH = 256
BLOCKS = DEPTH // CAP
LATE = 512
EDGE = GROUP_LAT * LON_DEV


def lanes(rows=1):
    return lax.broadcasted_iota(jnp.int32, (rows, 128), 1)


def pack_pair(pair, jac_ref, dep_ref, inv_ref, frac_ref, anch_ref, counts_ref):
    cols = pl.ds(pl.multiple_of(pair * 128, 128), 128)
    lane = lanes()
    first = lane < CAP
    limit = jnp.where(first, counts_ref[0, 2 * pair], counts_ref[0, 2 * pair + 1])
    live = (lane % CAP) < limit
    forcing = dep_ref[pl.ds(pair, 1), :] * inv_ref[pl.ds(pair, 1), :]
    top = jnp.where(live, jac_ref[0:136, cols].astype(F32) * forcing, 0.0)
    last = jnp.where(live, jac_ref[136:137, cols].astype(F32) * forcing, 0.0)
    a = frac_ref[0:1, cols]
    b = frac_ref[1:2, cols]
    lat = (anch_ref[0:1, cols] % LAT_DEV).astype(F32)
    lon = (anch_ref[1:2, cols] % LON_DEV).astype(F32)
    items = [last, (1.0 - a) * (1.0 - b), (1.0 - a) * b, a * (1.0 - b), a * b, lat, lon]
    row = lax.broadcasted_iota(jnp.int32, (8, 128), 0)
    tail = jnp.zeros((8, 128), F32)
    for n, item in enumerate(items):
        tail = jnp.where((row == n) & live, item, tail)
    low = top[0:HALF]
    high = jnp.concatenate([top[HALF:136], tail], axis=0)
    left = lanes(HALF) < CAP
    one = jnp.where(left, low, pltpu.roll(high, CAP, 1))
    two = jnp.where(left, pltpu.roll(low, CAP, 1), high)
    return one.astype(BF16), two.astype(BF16)


def unpack_pair(one, two):
    left = lanes(HALF) < CAP
    one = one.astype(F32)
    two = two.astype(F32)
    low = jnp.where(left, one, pltpu.roll(two, CAP, 1))
    high = jnp.where(left, pltpu.roll(one, CAP, 1), two)
    return jnp.concatenate([low, high], axis=0)


def spread(slots, lhs_ref, rhs_ref, at):
    cols = pl.ds(at, 128)
    info = slots[136:144]
    w00, w01, w10, w11 = (info[n : n + 1] for n in range(1, 5))
    lat, lon = info[5:6], info[6:7]
    group = jnp.floor(lat * (1.0 / GROUP_LAT))
    inner = lat - group * GROUP_LAT
    adj = slots.astype(BF16)
    for h in range(GROUPS):
        mask = jnp.where(group == h, 1.0, 0.0).astype(BF16)
        lhs_ref[h * ROWS : (h + 1) * ROWS, cols] = adj * mask
    j = lax.broadcasted_iota(jnp.int32, (LON_DEV, 128), 0).astype(F32)
    here = j == lon
    after = j == lon + 1.0
    near = jnp.where(here, w00, jnp.where(after, w01, 0.0)).astype(BF16)
    far = jnp.where(here, w10, jnp.where(after, w11, 0.0)).astype(BF16)
    for r in range(GROUP_LAT + 1):
        on_near = jnp.where(inner == r, 1.0, 0.0).astype(BF16)
        on_far = jnp.where(inner + 1.0 == r, 1.0, 0.0).astype(BF16)
        rhs_ref[r * LON_DEV : (r + 1) * LON_DEV, cols] = near * on_near + far * on_far
    edge = lon == LON_DEV - 1.0
    r = lax.broadcasted_iota(jnp.int32, (16, 128), 0).astype(F32)
    rim = jnp.where(edge & (r == inner), w01, jnp.where(edge & (r == inner + 1.0), w11, 0.0))
    rhs_ref[(GROUP_LAT + 1) * LON_DEV : (GROUP_LAT + 1) * LON_DEV + 16, cols] = rim.astype(BF16)


def place():
    band, lon = lax.axis_index("band"), lax.axis_index("lon")
    return lon, band // 8, band // 2 % 4, band % 2


def band_of(y, z, core):
    return (y * 4 + z) * 2 + core


ORDER = (
    (0, 0, 0, 0, 0),
    (0, 0, 0, 1, 1),
    (2, 2, 0, 0, 5),
    (2, 3, 0, 0, 4),
    (0, 1, 0, 0, 6),
    (3, 2, 0, 0, 8),
    (1, 0, 0, 0, 2),
    (1, 2, 0, 0, 10),
    (3, 0, 0, 0, 3),
    (2, 1, 0, 0, 12),
    (0, 3, 0, 0, 7),
    (1, 1, 0, 0, 11),
    (3, 3, 0, 0, 9),
    (3, 1, 0, 0, 16),
    (1, 3, 0, 0, 13),
    (2, 0, 0, 0, 14),
    (0, 2, 0, 0, 15),
    (0, 0, 2, 0, 98),
    (0, 0, 3, 0, 85),
    (0, 0, 1, 0, 91),
    (2, 2, 2, 0, 20),
    (3, 2, 2, 0, 19),
    (1, 0, 2, 0, 17),
    (1, 2, 2, 0, 21),
    (3, 0, 2, 0, 18),
    (2, 3, 2, 0, 23),
    (0, 1, 2, 0, 37),
    (2, 1, 2, 0, 26),
    (0, 3, 2, 0, 95),
    (3, 3, 2, 0, 22),
    (1, 1, 2, 0, 24),
    (3, 1, 2, 0, 27),
    (1, 3, 2, 0, 28),
    (2, 2, 3, 0, 30),
    (2, 2, 1, 0, 31),
    (0, 2, 2, 0, 48),
    (2, 0, 2, 0, 35),
    (2, 3, 3, 0, 33),
    (0, 1, 1, 0, 64),
    (2, 1, 1, 0, 32),
    (0, 3, 3, 0, 92),
    (1, 2, 3, 0, 39),
    (3, 0, 1, 0, 25),
    (3, 2, 1, 0, 38),
    (1, 0, 3, 0, 29),
    (2, 3, 1, 0, 40),
    (0, 1, 3, 0, 82),
    (3, 2, 3, 0, 41),
    (1, 0, 1, 0, 34),
    (2, 1, 3, 0, 44),
    (0, 3, 1, 0, 94),
    (1, 2, 1, 0, 43),
    (3, 0, 3, 0, 36),
    (1, 1, 1, 0, 42),
    (3, 3, 3, 0, 45),
    (1, 1, 3, 0, 51),
    (3, 3, 1, 0, 46),
    (0, 2, 3, 0, 63),
    (2, 0, 1, 0, 47),
    (1, 3, 3, 0, 52),
    (3, 1, 1, 0, 50),
    (3, 1, 3, 0, 55),
    (1, 3, 1, 0, 54),
    (2, 0, 3, 0, 56),
    (0, 2, 1, 0, 74),
    (2, 2, 2, 1, 60),
    (2, 2, 3, 1, 58),
    (0, 0, 1, 1, 109),
    (2, 1, 2, 1, 61),
    (0, 3, 0, 1, 90),
    (1, 2, 2, 1, 66),
    (3, 0, 0, 1, 49),
    (2, 2, 1, 1, 62),
    (0, 0, 3, 1, 96),
    (2, 3, 2, 1, 68),
    (0, 1, 0, 1, 87),
    (3, 2, 2, 1, 69),
    (1, 0, 0, 1, 53),
    (1, 2, 1, 1, 75),
    (3, 0, 3, 1, 59),
    (2, 3, 3, 1, 70),
    (0, 1, 1, 1, 108),
    (0, 2, 2, 1, 111),
    (2, 0, 0, 1, 57),
    (2, 2, 0, 1, 67),
    (0, 0, 2, 1, 126),
    (2, 1, 1, 1, 71),
    (0, 3, 3, 1, 93),
    (2, 0, 2, 1, 78),
    (0, 2, 0, 1, 110),
    (2, 1, 3, 1, 77),
    (0, 3, 1, 1, 112),
    (1, 1, 2, 1, 79),
    (3, 3, 0, 1, 65),
    (3, 2, 3, 1, 84),
    (1, 0, 1, 1, 72),
    (2, 3, 1, 1, 81),
    (0, 1, 3, 1, 113),
    (1, 2, 3, 1, 88),
    (3, 0, 1, 1, 73),
    (3, 2, 1, 1, 89),
    (1, 0, 3, 1, 80),
    (3, 3, 2, 1, 99),
    (1, 1, 0, 1, 76),
    (1, 3, 2, 1, 102),
    (3, 1, 0, 1, 83),
    (3, 1, 2, 1, 104),
    (1, 3, 0, 1, 86),
    (3, 3, 3, 1, 101),
    (1, 1, 1, 1, 100),
    (1, 0, 2, 1, 105),
    (3, 2, 0, 1, 97),
    (0, 2, 3, 1, 114),
    (2, 0, 1, 1, 103),
    (1, 1, 3, 1, 107),
    (3, 3, 1, 1, 106),
    (0, 2, 1, 1, 117),
    (2, 0, 3, 1, 118),
    (2, 3, 0, 1, 115),
    (0, 1, 2, 1, 123),
    (3, 1, 3, 1, 119),
    (1, 3, 1, 1, 121),
    (0, 3, 2, 1, 127),
    (2, 1, 0, 1, 116),
    (3, 1, 1, 1, 122),
    (1, 3, 3, 1, 124),
    (3, 0, 2, 1, 125),
    (1, 2, 0, 1, 120),
)


def main_kernel(
    jac_hbm, dep_hbm, inv_hbm, frac_hbm, anch_hbm, counts_hbm,
    out_ref,
    jac_ref, dep_ref, inv_ref, frac_ref, anch_ref, counts_ref, acc_ref, packed, recv, lhs_even, rhs_even, lhs_odd, rhs_odd, lhs_late, rhs_late, east, south, west, north, corner,
    load_sem, own_sem, send_sem, recv_sem, halo_send, halo_recv, z_sem, core_sem,
):
    x, y, z, core = place()
    barrier = pltpu.get_barrier_semaphore()
    plane = [
        (band_of((y + dy) % 4, z, core), (x + dx) % 4)
        for dx, dy in sorted({(n % 4, n // 4) for n in range(1, 16)})
    ]
    z_line = [(band_of(y, (z + d) % 4, core), x) for d in (1, 3, 2)]
    partner = [(band_of(y, z, 1 - core), x)]

    def greet(sem, devices):
        for device in devices:
            pl.semaphore_signal(sem, inc=1, device_id=device, device_id_type=MESH)

    def pack(first, last):
        def body(n, carry):
            band = band_of((y + n) % 4, (z + n // 4) % 4, (core + n // 16) % 2)
            for half in range(2):
                one, two = pack_pair(
                    2 * band + half, jac_ref, dep_ref, inv_ref, frac_ref, anch_ref, counts_ref
                )
                packed[n * 4 + 2 * half] = one
                packed[n * 4 + 2 * half + 1] = two
            return carry

        lax.fori_loop(first, last, body, 0)

    def block_copy(n):
        dx, dy, dz, dc, slot = ORDER[n]
        target = (x + dx) % 4
        return pltpu.make_async_remote_copy(
            src_ref=packed.at[(dc * 16 + dz * 4 + dy) * 4 + target],
            dst_ref=recv.at[slot],
            send_sem=send_sem.at[slot],
            recv_sem=recv_sem.at[slot],
            device_id=(band_of((y + dy) % 4, (z + dz) % 4, (core + dc) % 2), target),
            device_id_type=MESH,
        )

    def send(first, last):
        for n in range(first, last):
            block_copy(n).start()

    greet(barrier, plane + z_line + partner)
    loads = [
        pltpu.make_async_copy(source, held, load_sem.at[n])
        for n, (source, held) in enumerate(
            [
                (counts_hbm, counts_ref),
                (dep_hbm, dep_ref),
                (inv_hbm, inv_ref),
                (frac_hbm, frac_ref),
                (anch_hbm, anch_ref),
                (jac_hbm, jac_ref),
            ]
        )
    ]
    for load in loads:
        load.start()
    acc_ref[...] = jnp.zeros_like(acc_ref)
    for held in (rhs_even, rhs_odd, rhs_late):
        held[EDGE + LON_DEV : WIDE, :] = jnp.zeros((LON_DEV, held.shape[1]), BF16)
    for load in loads:
        load.wait()
    pack(0, 17)
    pl.semaphore_wait(barrier, 19)
    greet(z_sem, z_line)
    send(1, 17)
    pack(17, 22)
    pl.semaphore_wait(z_sem, 3)
    greet(core_sem, partner)
    send(17, 65)
    pl.semaphore_wait(core_sem, 1)
    pack(22, 32)
    own = pltpu.make_async_copy(packed.at[x], recv.at[0], own_sem)
    own.start()
    send(65, 128)

    def arrived(slot):
        pltpu.make_async_remote_copy(
            src_ref=packed.at[slot],
            dst_ref=recv.at[slot],
            send_sem=send_sem.at[slot],
            recv_sem=recv_sem.at[slot],
            device_id=partner[0],
            device_id_type=MESH,
        ).wait_recv()

    def fill(step, lhs_ref, rhs_ref, first=0):
        for n in range(first, BLOCKS):
            arrived(step * BLOCKS + n)
        for n in range(0, BLOCKS, 2):
            at = step * BLOCKS + n
            spread(unpack_pair(recv[at], recv[at + 1]), lhs_ref, rhs_ref, n * CAP)

    def add(lhs_ref, rhs_ref):
        acc_ref[...] += lax.dot_general(
            lhs_ref[...], rhs_ref[...], CONTRACT, preferred_element_type=F32
        )

    own.wait()
    fill(0, lhs_even, rhs_even, 1)
    early = (8192 - LATE) // DEPTH

    def body(t, carry):
        fill(2 * t + 1, lhs_odd, rhs_odd)
        add(lhs_even, rhs_even)
        fill(2 * t + 2, lhs_even, rhs_even)
        add(lhs_odd, rhs_odd)
        return carry

    lax.fori_loop(0, early // 2 - 1, body, 0)
    add(lhs_even, rhs_even)
    fill(early - 1, lhs_odd, rhs_odd)
    add(lhs_odd, rhs_odd)

    def collect(step, carry):
        for n in range(4):
            arrived(early * BLOCKS + step * 4 + n)
        for n in range(0, 4, 2):
            at = early * BLOCKS + step * 4 + n
            column = pl.multiple_of((step * 4 + n) * CAP, 128)
            spread(unpack_pair(recv[at], recv[at + 1]), lhs_late, rhs_late, column)
        return carry

    lax.fori_loop(0, LATE // CAP // 4, collect, 0)

    def late(n, carry):
        cols = pl.ds(pl.multiple_of(n * 256, 256), 256)
        acc_ref[:, cols] += lax.dot_general(
            lhs_late[...], rhs_late[cols, :], CONTRACT, preferred_element_type=F32
        )
        return carry

    lax.fori_loop(EDGE // 256, EDGE // 256 + 1, late, 0)

    rim = pl.ds(WIDE - LON_DEV, LON_DEV)
    total = acc_ref[0:ROWS, rim]
    for h in range(1, GROUPS):
        total = total + pltpu.roll(acc_ref[h * ROWS : (h + 1) * ROWS, rim], h * GROUP_LAT, 1)
    east[...] = total
    south[...] = acc_ref[(GROUPS - 1) * ROWS : GROUPS * ROWS, pl.ds(WIDE - 2 * LON_DEV, LON_DEV)]
    next_band = (band_of(y, z, core) + 1) % 32
    halos = []
    for n, (source, landing, device) in enumerate(
        [
            (south, north, (next_band, x)),
            (east, corner, (next_band, (x + 1) % 4)),
            (east, west, (band_of(y, z, core), (x + 1) % 4)),
        ]
    ):
        halos.append(
            pltpu.make_async_remote_copy(
                src_ref=source,
                dst_ref=landing,
                send_sem=halo_send.at[n],
                recv_sem=halo_recv.at[n],
                device_id=device,
                device_id_type=MESH,
            )
        )
    for copy in halos:
        copy.start()

    def own_row(i):
        h, r = i // GROUP_LAT, i % GROUP_LAT
        value = acc_ref[h * ROWS : (h + 1) * ROWS, r * LON_DEV : (r + 1) * LON_DEV]
        if r == 0 and h > 0:
            value = value + acc_ref[
                (h - 1) * ROWS : h * ROWS, GROUP_LAT * LON_DEV : (GROUP_LAT + 1) * LON_DEV
            ]
        return value

    lax.fori_loop(0, EDGE // 256, late, 0)
    for i in range(LAT_DEV):
        out_ref[pl.ds(i, LEV, stride=LAT_DEV), :] = own_row(i)[0:LEV]

    def drain(slot, carry):
        pltpu.make_async_remote_copy(
            src_ref=packed.at[slot],
            dst_ref=recv.at[slot],
            send_sem=send_sem.at[slot],
            recv_sem=recv_sem.at[slot],
            device_id=partner[0],
            device_id_type=MESH,
        ).wait_send()
        return carry

    lax.fori_loop(1, 128, drain, 0)
    for copy in halos:
        copy.wait()
    top = pl.ds(0, LEV, stride=LAT_DEV)
    side = jnp.where(lanes(LEV) == 0, corner[0:LEV, LAT_DEV : LAT_DEV + 1], 0.0)
    out_ref[top, :] += north[0:LEV] + side
    columns = jnp.transpose(west[...])[0:LAT_DEV]
    first = lanes(LAT_DEV) == 0
    for level in range(LEV):
        rows = pl.ds(level * LAT_DEV, LAT_DEV)
        out_ref[rows, :] += jnp.where(first, columns[:, level : level + 1], 0.0)


def per_device(jacobian, departure, inv_var, frac, anchors, counts):
    out = pl.pallas_call(
        main_kernel,
        out_shape=jax.ShapeDtypeStruct((LEV * LAT_DEV, LON_DEV), F32),
        in_specs=[pl.BlockSpec(memory_space=pltpu.HBM)] * 6,
        out_specs=pl.BlockSpec(memory_space=pltpu.VMEM),
        scratch_shapes=[
            pltpu.VMEM((LEV, 8192), BF16),
            pltpu.VMEM((64, 128), F32),
            pltpu.VMEM((64, 128), F32),
            pltpu.VMEM((2, 8192), F32),
            pltpu.VMEM((2, 8192), jnp.int32),
            pltpu.SMEM((1, 128), jnp.int32),
            pltpu.VMEM((GROUPS * ROWS, WIDE), F32),
            pltpu.VMEM((128, HALF, 128), BF16),
            pltpu.VMEM((128, HALF, 128), BF16),
            pltpu.VMEM((GROUPS * ROWS, DEPTH), BF16),
            pltpu.VMEM((WIDE, DEPTH), BF16),
            pltpu.VMEM((GROUPS * ROWS, DEPTH), BF16),
            pltpu.VMEM((WIDE, DEPTH), BF16),
            pltpu.VMEM((GROUPS * ROWS, LATE), BF16),
            pltpu.VMEM((WIDE, LATE), BF16),
        ]
        + [pltpu.VMEM((ROWS, LON_DEV), F32)] * 5
        + [
            pltpu.SemaphoreType.DMA((6,)),
            pltpu.SemaphoreType.DMA,
            pltpu.SemaphoreType.DMA((128,)),
            pltpu.SemaphoreType.DMA((128,)),
            pltpu.SemaphoreType.DMA((3,)),
            pltpu.SemaphoreType.DMA((3,)),
            pltpu.SemaphoreType.REGULAR,
            pltpu.SemaphoreType.REGULAR,
        ],
        compiler_params=pltpu.CompilerParams(
            collective_id=0, has_side_effects=True, vmem_limit_bytes=40 * 2**20
        ),
        name="exchange",
    )(
        *(
            pltpu.with_memory_space_constraint(value, pltpu.HBM)
            for value in (
                jacobian.T,
                departure.reshape(64, 128),
                inv_var.reshape(64, 128),
                frac,
                anchors,
                counts,
            )
        )
    )
    return out.reshape(LEV, LAT_DEV, LON_DEV)


def solution(mesh):
    return jax.shard_map(
        per_device,
        mesh=mesh,
        in_specs=(
            P(("band", "lon"), None),
            P(("band", "lon")),
            P(("band", "lon")),
            P(None, ("band", "lon")),
            P(None, ("band", "lon")),
            P(("band", "lon"), None),
        ),
        out_specs=P(None, "band", "lon"),
        check_vma=False,
    )
```

```python
import jax
import jax.numpy as jnp
from jax import lax
from jax.experimental import pallas as pl
from jax.experimental.pallas import tpu as pltpu
from jax.sharding import PartitionSpec as P

LEV = 137
LAT_DEV = 32
LON_DEV = 128
CAP = 64
ROWS = 144
HALF = ROWS // 2
GROUPS = 4
GROUP_LAT = LAT_DEV // GROUPS
WIDE = (GROUP_LAT + 2) * LON_DEV
F32 = jnp.float32
BF16 = jnp.bfloat16
MESH = pl.DeviceIdType.MESH
CONTRACT = (((1,), (1,)), ((), ()))
DEPTH = 256
BLOCKS = DEPTH // CAP
LATE = 512
EDGE = GROUP_LAT * LON_DEV


def lanes(rows=1):
    return lax.broadcasted_iota(jnp.int32, (rows, 128), 1)


def pack_pair(pair, jac_ref, dep_ref, inv_ref, frac_ref, anch_ref, counts_ref):
    cols = pl.ds(pl.multiple_of(pair * 128, 128), 128)
    lane = lanes()
    first = lane < CAP
    limit = jnp.where(first, counts_ref[0, 2 * pair], counts_ref[0, 2 * pair + 1])
    live = (lane % CAP) < limit
    forcing = dep_ref[pl.ds(pair, 1), :] * inv_ref[pl.ds(pair, 1), :]
    top = jnp.where(live, jac_ref[0:136, cols].astype(F32) * forcing, 0.0)
    last = jnp.where(live, jac_ref[136:137, cols].astype(F32) * forcing, 0.0)
    a = frac_ref[0:1, cols]
    b = frac_ref[1:2, cols]
    lat = (anch_ref[0:1, cols] % LAT_DEV).astype(F32)
    lon = (anch_ref[1:2, cols] % LON_DEV).astype(F32)
    items = [last, (1.0 - a) * (1.0 - b), (1.0 - a) * b, a * (1.0 - b), a * b, lat, lon]
    row = lax.broadcasted_iota(jnp.int32, (8, 128), 0)
    tail = jnp.zeros((8, 128), F32)
    for n, item in enumerate(items):
        tail = jnp.where((row == n) & live, item, tail)
    low = top[0:HALF]
    high = jnp.concatenate([top[HALF:136], tail], axis=0)
    left = lanes(HALF) < CAP
    one = jnp.where(left, low, pltpu.roll(high, CAP, 1))
    two = jnp.where(left, pltpu.roll(low, CAP, 1), high)
    return one.astype(BF16), two.astype(BF16)


def unpack_pair(one, two):
    left = lanes(HALF) < CAP
    one = one.astype(F32)
    two = two.astype(F32)
    low = jnp.where(left, one, pltpu.roll(two, CAP, 1))
    high = jnp.where(left, pltpu.roll(one, CAP, 1), two)
    return jnp.concatenate([low, high], axis=0)


def spread(slots, lhs_ref, rhs_ref, at):
    cols = pl.ds(at, 128)
    info = slots[136:144]
    w00, w01, w10, w11 = (info[n : n + 1] for n in range(1, 5))
    lat, lon = info[5:6], info[6:7]
    group = jnp.floor(lat * (1.0 / GROUP_LAT))
    inner = lat - group * GROUP_LAT
    adj = slots.astype(BF16)
    for h in range(GROUPS):
        mask = jnp.where(group == h, 1.0, 0.0).astype(BF16)
        lhs_ref[h * ROWS : (h + 1) * ROWS, cols] = adj * mask
    j = lax.broadcasted_iota(jnp.int32, (LON_DEV, 128), 0).astype(F32)
    here = j == lon
    after = j == lon + 1.0
    near = jnp.where(here, w00, jnp.where(after, w01, 0.0)).astype(BF16)
    far = jnp.where(here, w10, jnp.where(after, w11, 0.0)).astype(BF16)
    for r in range(GROUP_LAT + 1):
        on_near = jnp.where(inner == r, 1.0, 0.0).astype(BF16)
        on_far = jnp.where(inner + 1.0 == r, 1.0, 0.0).astype(BF16)
        rhs_ref[r * LON_DEV : (r + 1) * LON_DEV, cols] = near * on_near + far * on_far
    edge = lon == LON_DEV - 1.0
    r = lax.broadcasted_iota(jnp.int32, (16, 128), 0).astype(F32)
    rim = jnp.where(edge & (r == inner), w01, jnp.where(edge & (r == inner + 1.0), w11, 0.0))
    rhs_ref[(GROUP_LAT + 1) * LON_DEV : (GROUP_LAT + 1) * LON_DEV + 16, cols] = rim.astype(BF16)


def place():
    band, lon = lax.axis_index("band"), lax.axis_index("lon")
    return lon, band // 8, band // 2 % 4, band % 2


def band_of(y, z, core):
    return (y * 4 + z) * 2 + core


ORDER = (
    (0, 0, 0, 0, 0),
    (0, 0, 0, 1, 1),
    (2, 2, 0, 0, 5),
    (2, 3, 0, 0, 4),
    (0, 1, 0, 0, 6),
    (3, 2, 0, 0, 8),
    (1, 0, 0, 0, 2),
    (1, 2, 0, 0, 10),
    (3, 0, 0, 0, 3),
    (2, 1, 0, 0, 12),
    (0, 3, 0, 0, 7),
    (1, 1, 0, 0, 11),
    (3, 3, 0, 0, 9),
    (3, 1, 0, 0, 16),
    (1, 3, 0, 0, 13),
    (2, 0, 0, 0, 14),
    (0, 2, 0, 0, 15),
    (0, 0, 2, 0, 98),
    (0, 0, 3, 0, 85),
    (0, 0, 1, 0, 91),
    (2, 2, 2, 0, 20),
    (3, 2, 2, 0, 19),
    (1, 0, 2, 0, 17),
    (1, 2, 2, 0, 21),
    (3, 0, 2, 0, 18),
    (2, 3, 2, 0, 23),
    (0, 1, 2, 0, 37),
    (2, 1, 2, 0, 26),
    (0, 3, 2, 0, 95),
    (3, 3, 2, 0, 22),
    (1, 1, 2, 0, 24),
    (3, 1, 2, 0, 27),
    (1, 3, 2, 0, 28),
    (2, 2, 3, 0, 30),
    (2, 2, 1, 0, 31),
    (0, 2, 2, 0, 48),
    (2, 0, 2, 0, 35),
    (2, 3, 3, 0, 33),
    (0, 1, 1, 0, 64),
    (2, 1, 1, 0, 32),
    (0, 3, 3, 0, 92),
    (1, 2, 3, 0, 39),
    (3, 0, 1, 0, 25),
    (3, 2, 1, 0, 38),
    (1, 0, 3, 0, 29),
    (2, 3, 1, 0, 40),
    (0, 1, 3, 0, 82),
    (3, 2, 3, 0, 41),
    (1, 0, 1, 0, 34),
    (2, 1, 3, 0, 44),
    (0, 3, 1, 0, 94),
    (1, 2, 1, 0, 43),
    (3, 0, 3, 0, 36),
    (1, 1, 1, 0, 42),
    (3, 3, 3, 0, 45),
    (1, 1, 3, 0, 51),
    (3, 3, 1, 0, 46),
    (0, 2, 3, 0, 63),
    (2, 0, 1, 0, 47),
    (1, 3, 3, 0, 52),
    (3, 1, 1, 0, 50),
    (3, 1, 3, 0, 55),
    (1, 3, 1, 0, 54),
    (2, 0, 3, 0, 56),
    (0, 2, 1, 0, 74),
    (2, 2, 2, 1, 60),
    (2, 2, 3, 1, 58),
    (0, 0, 1, 1, 109),
    (2, 1, 2, 1, 61),
    (0, 3, 0, 1, 90),
    (1, 2, 2, 1, 66),
    (3, 0, 0, 1, 49),
    (2, 2, 1, 1, 62),
    (0, 0, 3, 1, 96),
    (2, 3, 2, 1, 68),
    (0, 1, 0, 1, 87),
    (3, 2, 2, 1, 69),
    (1, 0, 0, 1, 53),
    (1, 2, 1, 1, 75),
    (3, 0, 3, 1, 59),
    (2, 3, 3, 1, 70),
    (0, 1, 1, 1, 108),
    (0, 2, 2, 1, 111),
    (2, 0, 0, 1, 57),
    (2, 2, 0, 1, 67),
    (0, 0, 2, 1, 126),
    (2, 1, 1, 1, 71),
    (0, 3, 3, 1, 93),
    (2, 0, 2, 1, 78),
    (0, 2, 0, 1, 110),
    (2, 1, 3, 1, 77),
    (0, 3, 1, 1, 112),
    (1, 1, 2, 1, 79),
    (3, 3, 0, 1, 65),
    (3, 2, 3, 1, 84),
    (1, 0, 1, 1, 72),
    (2, 3, 1, 1, 81),
    (0, 1, 3, 1, 113),
    (1, 2, 3, 1, 88),
    (3, 0, 1, 1, 73),
    (3, 2, 1, 1, 89),
    (1, 0, 3, 1, 80),
    (3, 3, 2, 1, 99),
    (1, 1, 0, 1, 76),
    (1, 3, 2, 1, 102),
    (3, 1, 0, 1, 83),
    (3, 1, 2, 1, 104),
    (1, 3, 0, 1, 86),
    (3, 3, 3, 1, 101),
    (1, 1, 1, 1, 100),
    (1, 0, 2, 1, 105),
    (3, 2, 0, 1, 97),
    (0, 2, 3, 1, 114),
    (2, 0, 1, 1, 103),
    (1, 1, 3, 1, 107),
    (3, 3, 1, 1, 106),
    (0, 2, 1, 1, 117),
    (2, 0, 3, 1, 118),
    (2, 3, 0, 1, 115),
    (0, 1, 2, 1, 123),
    (3, 1, 3, 1, 119),
    (1, 3, 1, 1, 121),
    (0, 3, 2, 1, 127),
    (2, 1, 0, 1, 116),
    (3, 1, 1, 1, 122),
    (1, 3, 3, 1, 124),
    (3, 0, 2, 1, 125),
    (1, 2, 0, 1, 120),
)


def main_kernel(
    jac_hbm, dep_hbm, inv_hbm, frac_hbm, anch_hbm, counts_hbm,
    out_ref,
    jac_ref, dep_ref, inv_ref, frac_ref, anch_ref, counts_ref, acc_ref, packed, recv, lhs_even, rhs_even, lhs_odd, rhs_odd, lhs_late, rhs_late, east, south, west, north, corner,
    load_sem, own_sem, send_sem, recv_sem, halo_send, halo_recv, z_sem, core_sem,
):
    x, y, z, core = place()
    barrier = pltpu.get_barrier_semaphore()
    plane = [
        (band_of((y + dy) % 4, z, core), (x + dx) % 4)
        for dx, dy in sorted({(n % 4, n // 4) for n in range(1, 16)})
    ]
    z_line = [(band_of(y, (z + d) % 4, core), x) for d in (1, 3, 2)]
    partner = [(band_of(y, z, 1 - core), x)]

    def greet(sem, devices):
        for device in devices:
            pl.semaphore_signal(sem, inc=1, device_id=device, device_id_type=MESH)

    def pack(first, last):
        def body(n, carry):
            band = band_of((y + n) % 4, (z + n // 4) % 4, (core + n // 16) % 2)
            for half in range(2):
                one, two = pack_pair(
                    2 * band + half, jac_ref, dep_ref, inv_ref, frac_ref, anch_ref, counts_ref
                )
                packed[n * 4 + 2 * half] = one
                packed[n * 4 + 2 * half + 1] = two
            return carry

        lax.fori_loop(first, last, body, 0)

    def block_copy(n):
        dx, dy, dz, dc, slot = ORDER[n]
        target = (x + dx) % 4
        return pltpu.make_async_remote_copy(
            src_ref=packed.at[(dc * 16 + dz * 4 + dy) * 4 + target],
            dst_ref=recv.at[slot],
            send_sem=send_sem.at[slot],
            recv_sem=recv_sem.at[slot],
            device_id=(band_of((y + dy) % 4, (z + dz) % 4, (core + dc) % 2), target),
            device_id_type=MESH,
        )

    def send(first, last):
        for n in range(first, last):
            block_copy(n).start()

    greet(barrier, plane + z_line + partner)
    loads = [
        pltpu.make_async_copy(source, held, load_sem.at[n])
        for n, (source, held) in enumerate(
            [
                (counts_hbm, counts_ref),
                (dep_hbm, dep_ref),
                (inv_hbm, inv_ref),
                (frac_hbm, frac_ref),
                (anch_hbm, anch_ref),
                (jac_hbm, jac_ref),
            ]
        )
    ]
    for load in loads:
        load.start()
    acc_ref[...] = jnp.zeros_like(acc_ref)
    for held in (rhs_even, rhs_odd, rhs_late):
        held[EDGE + LON_DEV : WIDE, :] = jnp.zeros((LON_DEV, held.shape[1]), BF16)
    for load in loads:
        load.wait()
    pack(0, 17)
    pl.semaphore_wait(barrier, 19)
    greet(z_sem, z_line)
    send(1, 17)
    pack(17, 22)
    pl.semaphore_wait(z_sem, 3)
    greet(core_sem, partner)
    send(17, 65)
    pack(22, 32)
    pl.semaphore_wait(core_sem, 1)
    own = pltpu.make_async_copy(packed.at[x], recv.at[0], own_sem)
    own.start()
    send(65, 128)

    def arrived(slot):
        pltpu.make_async_remote_copy(
            src_ref=packed.at[slot],
            dst_ref=recv.at[slot],
            send_sem=send_sem.at[slot],
            recv_sem=recv_sem.at[slot],
            device_id=partner[0],
            device_id_type=MESH,
        ).wait_recv()

    def fill(step, lhs_ref, rhs_ref, first=0):
        for n in range(first, BLOCKS):
            arrived(step * BLOCKS + n)
        for n in range(0, BLOCKS, 2):
            at = step * BLOCKS + n
            spread(unpack_pair(recv[at], recv[at + 1]), lhs_ref, rhs_ref, n * CAP)

    def add(lhs_ref, rhs_ref):
        acc_ref[...] += lax.dot_general(
            lhs_ref[...], rhs_ref[...], CONTRACT, preferred_element_type=F32
        )

    own.wait()
    fill(0, lhs_even, rhs_even, 1)
    early = (8192 - LATE) // DEPTH

    def body(t, carry):
        fill(2 * t + 1, lhs_odd, rhs_odd)
        add(lhs_even, rhs_even)
        fill(2 * t + 2, lhs_even, rhs_even)
        add(lhs_odd, rhs_odd)
        return carry

    lax.fori_loop(0, early // 2 - 1, body, 0)
    add(lhs_even, rhs_even)
    fill(early - 1, lhs_odd, rhs_odd)
    add(lhs_odd, rhs_odd)

    def collect(step, carry):
        for n in range(4):
            arrived(early * BLOCKS + step * 4 + n)
        for n in range(0, 4, 2):
            at = early * BLOCKS + step * 4 + n
            column = pl.multiple_of((step * 4 + n) * CAP, 128)
            spread(unpack_pair(recv[at], recv[at + 1]), lhs_late, rhs_late, column)
        return carry

    lax.fori_loop(0, LATE // CAP // 4, collect, 0)

    def late(n, carry):
        cols = pl.ds(pl.multiple_of(n * 256, 256), 256)
        acc_ref[:, cols] += lax.dot_general(
            lhs_late[...], rhs_late[cols, :], CONTRACT, preferred_element_type=F32
        )
        return carry

    lax.fori_loop(EDGE // 256, EDGE // 256 + 1, late, 0)

    rim = pl.ds(WIDE - LON_DEV, LON_DEV)
    total = acc_ref[0:ROWS, rim]
    for h in range(1, GROUPS):
        total = total + pltpu.roll(acc_ref[h * ROWS : (h + 1) * ROWS, rim], h * GROUP_LAT, 1)
    east[...] = total
    south[...] = acc_ref[(GROUPS - 1) * ROWS : GROUPS * ROWS, pl.ds(WIDE - 2 * LON_DEV, LON_DEV)]
    next_band = (band_of(y, z, core) + 1) % 32
    halos = []
    for n, (source, landing, device) in enumerate(
        [
            (south, north, (next_band, x)),
            (east, corner, (next_band, (x + 1) % 4)),
            (east, west, (band_of(y, z, core), (x + 1) % 4)),
        ]
    ):
        halos.append(
            pltpu.make_async_remote_copy(
                src_ref=source,
                dst_ref=landing,
                send_sem=halo_send.at[n],
                recv_sem=halo_recv.at[n],
                device_id=device,
                device_id_type=MESH,
            )
        )
    for copy in halos:
        copy.start()

    def own_row(i):
        h, r = i // GROUP_LAT, i % GROUP_LAT
        value = acc_ref[h * ROWS : (h + 1) * ROWS, r * LON_DEV : (r + 1) * LON_DEV]
        if r == 0 and h > 0:
            value = value + acc_ref[
                (h - 1) * ROWS : h * ROWS, GROUP_LAT * LON_DEV : (GROUP_LAT + 1) * LON_DEV
            ]
        return value

    lax.fori_loop(0, EDGE // 256, late, 0)
    for i in range(LAT_DEV):
        out_ref[pl.ds(i, LEV, stride=LAT_DEV), :] = own_row(i)[0:LEV]

    def drain(slot, carry):
        pltpu.make_async_remote_copy(
            src_ref=packed.at[slot],
            dst_ref=recv.at[slot],
            send_sem=send_sem.at[slot],
            recv_sem=recv_sem.at[slot],
            device_id=partner[0],
            device_id_type=MESH,
        ).wait_send()
        return carry

    lax.fori_loop(1, 128, drain, 0)
    for copy in halos:
        copy.wait()
    top = pl.ds(0, LEV, stride=LAT_DEV)
    side = jnp.where(lanes(LEV) == 0, corner[0:LEV, LAT_DEV : LAT_DEV + 1], 0.0)
    out_ref[top, :] += north[0:LEV] + side
    columns = jnp.transpose(west[...])[0:LAT_DEV]
    first = lanes(LAT_DEV) == 0
    for level in range(LEV):
        rows = pl.ds(level * LAT_DEV, LAT_DEV)
        out_ref[rows, :] += jnp.where(first, columns[:, level : level + 1], 0.0)


def per_device(jacobian, departure, inv_var, frac, anchors, counts):
    out = pl.pallas_call(
        main_kernel,
        out_shape=jax.ShapeDtypeStruct((LEV * LAT_DEV, LON_DEV), F32),
        in_specs=[pl.BlockSpec(memory_space=pltpu.HBM)] * 6,
        out_specs=pl.BlockSpec(memory_space=pltpu.VMEM),
        scratch_shapes=[
            pltpu.VMEM((LEV, 8192), BF16),
            pltpu.VMEM((64, 128), F32),
            pltpu.VMEM((64, 128), F32),
            pltpu.VMEM((2, 8192), F32),
            pltpu.VMEM((2, 8192), jnp.int32),
            pltpu.SMEM((1, 128), jnp.int32),
            pltpu.VMEM((GROUPS * ROWS, WIDE), F32),
            pltpu.VMEM((128, HALF, 128), BF16),
            pltpu.VMEM((128, HALF, 128), BF16),
            pltpu.VMEM((GROUPS * ROWS, DEPTH), BF16),
            pltpu.VMEM((WIDE, DEPTH), BF16),
            pltpu.VMEM((GROUPS * ROWS, DEPTH), BF16),
            pltpu.VMEM((WIDE, DEPTH), BF16),
            pltpu.VMEM((GROUPS * ROWS, LATE), BF16),
            pltpu.VMEM((WIDE, LATE), BF16),
        ]
        + [pltpu.VMEM((ROWS, LON_DEV), F32)] * 5
        + [
            pltpu.SemaphoreType.DMA((6,)),
            pltpu.SemaphoreType.DMA,
            pltpu.SemaphoreType.DMA((128,)),
            pltpu.SemaphoreType.DMA((128,)),
            pltpu.SemaphoreType.DMA((3,)),
            pltpu.SemaphoreType.DMA((3,)),
            pltpu.SemaphoreType.REGULAR,
            pltpu.SemaphoreType.REGULAR,
        ],
        compiler_params=pltpu.CompilerParams(
            collective_id=0, has_side_effects=True, vmem_limit_bytes=40 * 2**20
        ),
        name="exchange",
    )(
        *(
            pltpu.with_memory_space_constraint(value, pltpu.HBM)
            for value in (
                jacobian.T,
                departure.reshape(64, 128),
                inv_var.reshape(64, 128),
                frac,
                anchors,
                counts,
            )
        )
    )
    return out.reshape(LEV, LAT_DEV, LON_DEV)


def solution(mesh):
    return jax.shard_map(
        per_device,
        mesh=mesh,
        in_specs=(
            P(("band", "lon"), None),
            P(("band", "lon")),
            P(("band", "lon")),
            P(None, ("band", "lon")),
            P(None, ("band", "lon")),
            P(("band", "lon"), None),
        ),
        out_specs=P(None, "band", "lon"),
        check_vma=False,
    )
```
